32 devices in a mesh: grp: 2 (over x), row: 16 (over z, y, core).
Axes of the slice: x: 2, y: 2, z: 4, core: 2. Of those that a mesh axis runs over, the one named last changes fastest.
Arguments:
- members_in: bfloat16 [256, 4096], P(('grp', 'row')), parts along dimension 0, may hold values from -6 to 6
- gate_up: bfloat16 [4096, 2, 14336], P(None, None, 'row'), may hold values from -0.09375 to 0.09375
- down_weight: bfloat16 [14336, 4096], P('row'), may hold values from -0.046875 to 0.046875
- factor_in: bfloat16 [256, 4, 4096], P('grp', None, 'row'), parts along dimension 0, may hold values from -0.09375 to 0.09375
- factor_out: bfloat16 [256, 4, 2, 14336], P('grp', None, None, 'row'), parts along dimension 0, may hold values from -6 to 6
- target: float32 [256, 4096], P(('grp', 'row')), parts along dimension 0, may hold values from -6 to 6
Outputs:
- outputs: bfloat16 [256, 4096], P(('grp', 'row')), parts along dimension 0
- fitness: float32 [256], P(('grp', 'row')), parts along dimension 0
- update: float32 [8192, 2, 14336], P('grp', None, 'row'), parts along dimension 0
The draws below stay inside these ranges and needn't reach their ends.
There are 2 independent parts, one for each index of `grp`. The reference program is written for one: setup_inputs(seed, part) draws one part's arguments, and reference() takes and returns one part's arrays. A program takes and returns all parts, laid end to end along the dimension named above; an argument that names none is the same for every part. Nothing has to cross between parts.
All inputs are finite; a program needn't handle non-finite values.
Results may differ from the reference program's by a relative error of at most 0.0049.
Values may be sent and summed in bfloat16 or wider, within the bound.
A program may use at most 128 MiB of HBM per device.

```python
import math
import jax
import jax.numpy as jnp
from jax import lax

D = 4096
FF = 14336
RANK = 4
MEMBERS = 128


def draw_target(key, part):
    base_key = jax.random.fold_in(key, 7001)
    first, second = jax.random.split(base_key)
    places = jnp.arange(MEMBERS).astype(jnp.float32) / max(MEMBERS - 1, 1)
    jitter = jnp.exp(jax.random.uniform(second, (MEMBERS,), jnp.float32, -0.22, 0.22))
    values = jnp.clip(jax.random.normal(first, (MEMBERS, D), jnp.float32), -3.0, 3.0)
    ramp = 0.5 + places
    return (values * (ramp * jitter)[:, None]).astype(jnp.float32)


def block_levels(rng, shape, cuts, low, high):
    level = 1.0
    for position, shards_of in cuts:
        heights = jax.random.uniform(jax.random.fold_in(jax.random.fold_in(rng, 6), position), (shards_of,), jnp.float32, low / len(cuts), high / len(cuts))
        level = level * jnp.repeat(jnp.exp(heights), shape[position] // shards_of).reshape((-1,) + (1,) * (len(shape) - 1 - position))
    return level


def gaussian(rng, extent, deviation, limit, cuts=(), kind=jnp.bfloat16):
    result = jax.random.normal(rng, extent, jnp.float32) * deviation
    if len(cuts) > 0:
        result = block_levels(rng, extent, cuts, -0.22, 0.18) * result
    return jnp.clip(result, min=-limit, max=limit).astype(kind)


def setup_inputs(seed: int = 0, part: int = 0) -> dict:
    key_list = jax.random.split(jax.random.key(seed), 7)
    own_keys = jax.random.split(jax.random.fold_in(key_list[6], part), 7)
    return {
        "members_in": gaussian(own_keys[0], (MEMBERS, D), 1.0, 6.0, ((0, 16),)),
        "gate_up": gaussian(key_list[1], (D, 2, FF), D ** -0.5, 0.09375, ((2, 16),)),
        "down_weight": gaussian(key_list[2], (FF, D), FF ** -0.5, 0.046875, ((0, 16),)),
        "factor_in": gaussian(own_keys[3], (MEMBERS, RANK, D), D ** -0.5, 0.09375, ((2, 16),)),
        "factor_out": gaussian(own_keys[4], (MEMBERS, RANK, 2, FF), 1.0, 6.0, ((3, 16),)),
        "target": draw_target(jax.random.fold_in(jax.random.fold_in(key_list[6], part), 71), part),
    }


noise_scale = 0.5

def reference(members_in, gate_up, down_weight, factor_in, factor_out, target):
    highest = lax.Precision.HIGHEST
    inputs = members_in.astype(jnp.float32)
    factor_a = factor_in.astype(jnp.float32)
    factor_b = factor_out.astype(jnp.float32)
    projected = jnp.einsum('md,mrd->mr', inputs, factor_a, precision=highest)
    stacked = jnp.dot(inputs, gate_up.reshape(D, 2 * FF).astype(jnp.float32), precision=highest)
    stacked = stacked.reshape(MEMBERS, 2, FF)
    noise = jnp.einsum('mr,mrkf->mkf', projected, factor_b, precision=highest)
    stacked = stacked + noise * (noise_scale / math.sqrt(RANK))
    hidden = (jax.nn.silu(stacked[:, 0]) * stacked[:, 1]).astype(jnp.bfloat16)
    sums = jnp.dot(hidden.astype(jnp.float32), down_weight.astype(jnp.float32), precision=highest)
    losses = lax.optimization_barrier(jnp.mean((sums - target) ** 2, axis=1))
    average = jnp.mean(losses)
    spread = jnp.mean((losses - average) ** 2)
    fitness = (average - losses) / jnp.sqrt(spread + 1e-06)
    scaled = (fitness[:, None, None, None] * factor_b).astype(jnp.bfloat16)
    update = lax.dot_general(factor_a, scaled.astype(jnp.float32), (((0, 1), (0, 1)), ((), ())), precision=highest)
    update = update * math.sqrt(D / (MEMBERS * RANK))
    return (sums.astype(jnp.bfloat16), fitness, update)
```

```python
import functools
import math

import jax
import jax.numpy as jnp
from jax import lax
from jax.experimental import pallas as pl
from jax.experimental.pallas import tpu as pltpu
from jax.sharding import PartitionSpec as P

noise_scale = 0.5
MESH = pl.DeviceIdType.MESH
LANES = 128
VMEM_LIMIT = 62 * 1024 * 1024


class Gather:
    def __init__(self, depth, place, own, slots, send_sems, recv_sems, local_sem):
        self.depth, self.place = depth, place
        self.own, self.slots = own, slots
        self.send_sems, self.recv_sems, self.local_sem = send_sems, recv_sems, local_sem
        self.sent = []

    def index(self, z, y, c):
        return (z * 2 + y) * 2 + c

    def copy(self, source, origin, target):
        sem = self.send_sems.at[len(self.sent)]
        return pltpu.make_async_remote_copy(
            src_ref=source,
            dst_ref=self.slots.at[origin],
            send_sem=sem,
            recv_sem=self.recv_sems.at[origin],
            device_id={"row": target},
            device_id_type=MESH,
        )

    def send(self, source, origin, target, condition):
        copy = self.copy(source, origin, target)
        self.sent.append((condition, copy))
        if condition is None:
            copy.start()
        else:
            pl.when(condition)(copy.start)

    def arrive(self, origin, condition):
        z, y, c = self.place
        copy = pltpu.make_async_remote_copy(
            src_ref=self.slots.at[origin],
            dst_ref=self.slots.at[origin],
            send_sem=self.send_sems.at[0],
            recv_sem=self.recv_sems.at[origin],
            device_id={"row": self.index(z, y, 1 - c)},
            device_id_type=MESH,
        )
        if condition is None:
            copy.wait_recv()
        else:
            pl.when(condition)(copy.wait_recv)

    def start(self):
        z, y, c = self.place
        me = self.index(z, y, c)
        self.local = pltpu.make_async_copy(self.own, self.slots.at[me], self.local_sem)
        self.local.start()
        up, down = z + 1 < self.depth, z >= 1
        self.send(self.own, me, self.index(jnp.minimum(z + 1, self.depth - 1), y, c), up)
        self.send(self.own, me, self.index(jnp.maximum(z - 1, 0), y, c), down)
        self.send(self.own, me, self.index(z, 1 - y, c), None)
        self.send(self.own, me, self.index(z, y, 1 - c), None)

    def along_z(self, step):
        z, y, c = self.place
        for sign in (-1, 1):
            at = z + sign * (1 + step)
            here = (at >= 0) & (at < self.depth)
            origin = self.index(jnp.clip(at, 0, self.depth - 1), y, c)
            self.arrive(origin, here)
            on = z - sign
            further = here & (on >= 0) & (on < self.depth)
            source = self.slots.at[origin]
            if step < self.depth - 2:
                self.send(
                    source, origin, self.index(jnp.clip(on, 0, self.depth - 1), y, c), further
                )
            self.send(source, origin, self.index(z, 1 - y, c), here)
            self.send(source, origin, self.index(z, y, 1 - c), here)

    def along_y(self, step):
        z, y, c = self.place
        for sign in (-1, 1) if step else (1,):
            at = z + sign * step
            here = (at >= 0) & (at < self.depth) if step else None
            origin = self.index(jnp.clip(at, 0, self.depth - 1), 1 - y, c)
            self.arrive(origin, here)
            self.send(self.slots.at[origin], origin, self.index(z, y, 1 - c), here)

    def finish(self):
        z, y, c = self.place
        for at in range(self.depth):
            for side in range(2):
                self.arrive(self.index(at, side, 1 - c), None)
        self.local.wait()

    def drain(self):
        for condition, copy in self.sent:
            if condition is None:
                copy.wait_send()
            else:
                pl.when(condition)(copy.wait_send)


def sends_of(depth):
    return 4 + 6 * (depth - 1) + 2 * depth


def forward_kernel(
    n, rank, chunks, lag,
    x_ref, factor_ref, target_ref, gate_up_ref, down_ref, out_factor_ref,
    outputs_ref, fitness_ref, all_fitness_ref, full_factor_ref, noise_ref,
    weights, down, raw, wide, x_all, x_mixed, acc, hidden, proj_in, proj_out, loss_in, loss_out,
    pair_out, pair_keep, pair_in, y_out, y_keep, y_in, z_out, z_keep, z_in, sums,
    weight_sems, down_sem, raw_sems, local_sems,
    x_send, x_recv, f_send, f_recv, p_send, p_recv, l_send, l_recv,
    c_send, c_recv, y_send, y_recv, z_send, z_recv,
):
    depth = n // 4
    me = lax.axis_index("row")
    c = lax.rem(me, 2)
    y = lax.rem(me // 2, 2)
    z = me // 4
    own_rows, width = x_ref.shape
    members = n * own_rows
    local_width = factor_ref.shape[0]
    blocks = weights.shape[0]

    loads = []
    for j in range(blocks):
        cut = pl.ds(j * LANES, LANES)
        raw_copy = pltpu.make_async_copy(out_factor_ref.at[:, :, cut], raw.at[j], raw_sems.at[j])
        raw_copy.start()
        loads.append(raw_copy)
    weight_loads = []
    for j in range(blocks):
        cut = pl.ds(j * LANES, LANES)
        copy = pltpu.make_async_copy(gate_up_ref.at[:, :, cut], weights.at[j], weight_sems.at[j])
        copy.start()
        weight_loads.append(copy)
    down_load = pltpu.make_async_copy(down_ref, down, down_sem)
    down_load.start()

    barrier = pltpu.get_barrier_semaphore()
    for k in range(1, n):
        pl.semaphore_signal(
            barrier, inc=1, device_id={"row": lax.rem(me + k, n)}, device_id_type=MESH
        )
    pl.semaphore_wait(barrier, n - 1)

    x_gather = Gather(depth, (z, y, c), x_ref, x_all, x_send, x_recv, local_sems.at[0])
    f_gather = Gather(
        depth, (z, y, c), factor_ref, full_factor_ref, f_send, f_recv, local_sems.at[1]
    )
    x_gather.start()

    def split(j):
        loads[j].wait()
        wide[...] = raw.at[j].reshape(members * rank * 2, LANES)[...].astype(jnp.float32)
        for r in range(rank):
            for k in range(2):
                part = wide[pl.ds(r * 2 + k, members, 2 * rank), :]
                noise_ref[j, r * members:(r + 1) * members, k * LANES:(k + 1) * LANES] = (
                    part.astype(jnp.bfloat16)
                )

    for step in range(depth - 1):
        x_gather.along_z(step)
        x_gather.along_y(step)
        split(step)
    x_gather.along_y(depth - 1)
    x_gather.finish()
    f_gather.start()

    def to_all(source, slots, send_sems, recv_sems):
        copies = []
        for k in range(1, n):
            copy = pltpu.make_async_remote_copy(
                src_ref=source,
                dst_ref=slots.at[k],
                send_sem=send_sems.at[k],
                recv_sem=recv_sems.at[k],
                device_id={"row": lax.rem(me + k, n)},
                device_id_type=MESH,
            )
            copy.start()
            copies.append(copy)
        return copies

    own_columns = pl.ds(pl.multiple_of(me * local_width, LANES), local_width)
    x_own = x_all[:, :, own_columns].reshape(members, local_width)
    crossed = jnp.dot(x_own, factor_ref[...], preferred_element_type=jnp.float32)
    row_at = lax.broadcasted_iota(jnp.int32, (members, members), 0)
    lane_at = lax.broadcasted_iota(jnp.int32, (members, members), 1)
    proj_out[...] = jnp.zeros_like(proj_out)
    for r in range(rank):
        block = crossed[:, r * members:(r + 1) * members]
        proj_out[r:r + 1, :] = jnp.sum(
            jnp.where(row_at == lane_at, block, 0.0), axis=0, keepdims=True
        )
    proj_copies = to_all(proj_out, proj_in, p_send, p_recv)

    spread_row = lax.broadcasted_iota(jnp.int32, (LANES, 2 * LANES), 0)
    spread_lane = lax.broadcasted_iota(jnp.int32, (LANES, 2 * LANES), 1)
    to_gate = jnp.where(spread_lane == 2 * spread_row, 1.0, 0.0).astype(jnp.bfloat16)
    to_up = jnp.where(spread_lane == 2 * spread_row + 1, 1.0, 0.0).astype(jnp.bfloat16)

    @pl.loop(0, width // LANES)
    def _(i):
        piece = x_all[:, :, pl.ds(pl.multiple_of(i * LANES, LANES), LANES)]
        piece = piece.reshape(members, LANES)
        cut = pl.ds(pl.multiple_of(i * 2 * LANES, LANES), 2 * LANES)
        x_mixed[0:members, cut] = jnp.dot(
            piece, to_gate, preferred_element_type=jnp.float32
        ).astype(jnp.bfloat16)
        x_mixed[members:2 * members, cut] = jnp.dot(
            piece, to_up, preferred_element_type=jnp.float32
        ).astype(jnp.bfloat16)

    for j in range(depth - 1, blocks):
        split(j)

    for copy in proj_copies:
        copy.wait()
    projected = proj_out[...]
    for k in range(1, n):
        projected = projected + proj_in[k]
    columns = [
        jnp.sum(
            jnp.where(row_at == lane_at, projected[r:r + 1, :], 0.0), axis=1, keepdims=True
        )
        for r in range(rank)
    ]

    deep = 2 * width // 8
    for first in range(0, blocks, 2):
        group = list(range(first, min(first + 2, blocks)))
        for j in group:
            weight_loads[j].wait()
        views = [weights.at[j].reshape(2 * width, LANES) for j in group]
        span = len(group) * LANES
        acc[...] = jnp.zeros_like(acc)

        @pl.loop(0, 2 * width // deep)
        def _(i):
            rows = pl.ds(pl.multiple_of(i * deep, LANES), deep)
            w = [view[rows, :] for view in views]
            w = jnp.concatenate(w, axis=1) if len(w) > 1 else w[0]
            acc[:, 0:span] += jnp.dot(
                x_mixed[:, rows], w, preferred_element_type=jnp.float32
            )

        for at, j in enumerate(group):
            lanes = slice(at * LANES, (at + 1) * LANES)
            two = []
            for k in range(2):
                noise = jnp.zeros((members, LANES), jnp.float32)
                for r in range(rank):
                    noise += columns[r] * noise_ref[
                        j, r * members:(r + 1) * members, k * LANES:(k + 1) * LANES
                    ].astype(jnp.float32)
                two.append(
                    acc[k * members:(k + 1) * members, lanes]
                    + noise * (noise_scale / math.sqrt(rank))
                )
            hidden[:, j * LANES:(j + 1) * LANES] = (
                (two[0] / (1.0 + jnp.exp(-two[0]))) * two[1]
            ).astype(jnp.bfloat16)

    f_gather.along_z(0)
    f_gather.along_y(0)
    down_load.wait()

    span = width // chunks
    sibling, across = (z * 2 + y) * 2 + 1 - c, (z * 2 + 1 - y) * 2 + c
    pair_copies, y_copies, z_copies = [], [], []

    def down_step(i):
        part = jnp.dot(
            hidden[...], down[:, i * span:(i + 1) * span], preferred_element_type=jnp.float32
        ).reshape(2 * depth, 2, own_rows, span)
        first, second = part[:, 0], part[:, 1]
        pair_keep[i] = jnp.where(c == 0, first, second)
        pair_out[i] = jnp.where(c == 0, second, first)
        copy = pltpu.make_async_remote_copy(
            src_ref=pair_out.at[i], dst_ref=pair_in.at[i],
            send_sem=c_send.at[i], recv_sem=c_recv.at[i],
            device_id={"row": sibling}, device_id_type=MESH,
        )
        copy.start()
        pair_copies.append(copy)

    def y_step(i):
        pair_copies[i].wait_recv()
        part = (pair_keep[i] + pair_in[i]).reshape(depth, 2, own_rows, span)
        first, second = part[:, 0], part[:, 1]
        y_keep[i] = jnp.where(y == 0, first, second)
        y_out[i] = (
            jnp.where(y == 0, second, first).reshape(depth * own_rows, span).astype(jnp.bfloat16)
        )
        copy = pltpu.make_async_remote_copy(
            src_ref=y_out.at[i], dst_ref=y_in.at[i],
            send_sem=y_send.at[i], recv_sem=y_recv.at[i],
            device_id={"row": across}, device_id_type=MESH,
        )
        copy.start()
        y_copies.append(copy)

    def z_step(i):
        y_copies[i].wait_recv()
        part = y_keep[i] + y_in[i].astype(jnp.float32).reshape(depth, own_rows, span)
        z_keep[i] = part
        z_out[i] = part.astype(jnp.bfloat16)
        copies = []
        for k in range(1, depth):
            to = lax.rem(z + k, depth)
            copy = pltpu.make_async_remote_copy(
                src_ref=z_out.at[i, to], dst_ref=z_in.at[i, k],
                send_sem=z_send.at[i, k], recv_sem=z_recv.at[i, k],
                device_id={"row": (to * 2 + y) * 2 + c}, device_id_type=MESH,
            )
            copy.start()
            copies.append(copy)
        z_copies.append(copies)

    for t in range(chunks + 2 * lag):
        if t < chunks:
            down_step(t)
        if 0 <= t - lag < chunks:
            y_step(t - lag)
        if 0 <= t - 2 * lag < chunks:
            z_step(t - 2 * lag)
        if t == chunks - 1:
            for step in range(1, depth - 1):
                f_gather.along_z(step)
                f_gather.along_y(step)

    total = jnp.zeros((own_rows, 1), jnp.float32)
    for i in range(chunks):
        part = z_keep[i, z]
        for k in range(1, depth):
            z_copies[i][k - 1].wait_recv()
            part = part + z_in[i, k].astype(jnp.float32)
        cut = slice(i * span, (i + 1) * span)
        outputs_ref[:, cut] = part.astype(jnp.bfloat16)
        miss = part - target_ref[:, cut]
        total = total + jnp.sum(miss * miss, axis=1, keepdims=True)
    loss_out[...] = jnp.broadcast_to(total / width, loss_out.shape)
    loss_copies = to_all(loss_out, loss_in, l_send, l_recv)
    f_gather.along_y(depth - 1)
    for copy in loss_copies:
        copy.wait()
    loss_in[0] = loss_out[...]

    def by_member(slot):
        return loss_in[slot]

    average = jnp.zeros((1, LANES), jnp.float32)
    for k in range(n):
        average = average + jnp.sum(loss_in[k], axis=0, keepdims=True)
    average = average / members
    spread = jnp.zeros((1, LANES), jnp.float32)
    for k in range(n):
        away = loss_in[k] - average
        spread = spread + jnp.sum(away * away, axis=0, keepdims=True)
    scale = jnp.sqrt(spread / members + 1e-06)
    for d in range(n):
        slot = lax.rem(me - d + n, n)
        all_fitness_ref[d * own_rows:(d + 1) * own_rows, :] = (
            average - loss_in[slot]
        ) / scale
    fitness_ref[...] = (average - loss_in[0]) / scale

    f_gather.finish()
    x_gather.drain()
    f_gather.drain()
    for copy in pair_copies + y_copies + [copy for some in z_copies for copy in some]:
        copy.wait_send()


def update_kernel(scale, rank, factor_ref, noise_ref, fitness_ref, update_ref, scaled):
    members = fitness_ref.shape[0]
    rows = update_ref.shape[0]

    @pl.when(pl.program_id(1) == 0)
    def _():
        fitness = fitness_ref[...]
        for r in range(rank):
            for k in range(2):
                at = (slice(r * members, (r + 1) * members), slice(k * LANES, (k + 1) * LANES))
                scaled[at] = (
                    fitness * noise_ref[(0,) + at].astype(jnp.float32)
                ).astype(jnp.bfloat16)

    start = pl.multiple_of(pl.program_id(1) * rows, LANES)
    result = jnp.dot(
        factor_ref[pl.ds(start, rows), :], scaled[...], preferred_element_type=jnp.float32
    ) * scale
    view = update_ref.reshape(2 * rows, LANES)
    view[pl.ds(0, rows, 2), :] = result[:, :LANES]
    view[pl.ds(1, rows, 2), :] = result[:, LANES:]


def fast_body(n, members_in, gate_up, down_weight, factor_in, factor_out, target):
    own_rows, width = members_in.shape
    local_units = gate_up.shape[2]
    members, rank, local_width = factor_in.shape
    blocks = local_units // LANES
    depth = n // 4
    chunks, lag = 8, 2
    span = width // chunks
    factor = factor_in.transpose(2, 1, 0).reshape(local_width, rank * members)
    rows_out = factor_out.reshape(members * rank, 2, local_units)
    bf16, f32 = jnp.bfloat16, jnp.float32
    dma = pltpu.SemaphoreType.DMA
    vmem = pl.BlockSpec(memory_space=pltpu.VMEM)
    hbm = pl.BlockSpec(memory_space=pl.ANY)
    outputs, fitness, all_fitness, full_factor, noise = pl.pallas_call(
        functools.partial(forward_kernel, n, rank, chunks, lag),
        out_shape=(
            jax.ShapeDtypeStruct((own_rows, width), bf16),
            jax.ShapeDtypeStruct((own_rows, LANES), f32),
            jax.ShapeDtypeStruct((members, LANES), f32),
            jax.ShapeDtypeStruct((n, local_width, rank * members), bf16),
            jax.ShapeDtypeStruct((blocks, rank * members, 2 * LANES), bf16),
        ),
        in_specs=[vmem, vmem, vmem, hbm, hbm, hbm],
        out_specs=(vmem, vmem, vmem, hbm, vmem),
        scratch_shapes=[
            pltpu.VMEM((blocks, width, 2, LANES), bf16),
            pltpu.VMEM((local_units, width), bf16),
            pltpu.VMEM((blocks, members * rank, 2, LANES), bf16),
            pltpu.VMEM((members * rank * 2, LANES), f32),
            pltpu.VMEM((n, own_rows, width), bf16),
            pltpu.VMEM((2 * members, 2 * width), bf16),
            pltpu.VMEM((2 * members, 2 * LANES), f32),
            pltpu.VMEM((members, local_units), bf16),
            pltpu.VMEM((n, 8, members), f32),
            pltpu.VMEM((8, members), f32),
            pltpu.VMEM((n, own_rows, LANES), f32),
            pltpu.VMEM((own_rows, LANES), f32),
            pltpu.VMEM((chunks, 2 * depth, own_rows, span), f32),
            pltpu.VMEM((chunks, 2 * depth, own_rows, span), f32),
            pltpu.VMEM((chunks, 2 * depth, own_rows, span), f32),
            pltpu.VMEM((chunks, depth * own_rows, span), bf16),
            pltpu.VMEM((chunks, depth, own_rows, span), f32),
            pltpu.VMEM((chunks, depth * own_rows, span), bf16),
            pltpu.VMEM((chunks, depth, own_rows, span), bf16),
            pltpu.VMEM((chunks, depth, own_rows, span), f32),
            pltpu.VMEM((chunks, depth, own_rows, span), bf16),
            pltpu.VMEM((8, LANES), f32),
            dma((blocks,)), dma(()), dma((blocks,)), dma((2,)),
            dma((sends_of(depth),)), dma((n,)),
            dma((sends_of(depth),)), dma((n,)),
            dma((n,)), dma((n,)), dma((n,)), dma((n,)),
            dma((chunks,)), dma((chunks,)), dma((chunks,)), dma((chunks,)),
            dma((chunks, depth)), dma((chunks, depth)),
        ],
        compiler_params=pltpu.CompilerParams(
            collective_id=0, has_side_effects=True, vmem_limit_bytes=VMEM_LIMIT
        ),
        name="forward",
    )(members_in, factor, target, gate_up, down_weight, rows_out)

    block = width // 4
    step_scale = math.sqrt(width / (members * rank))
    update = pl.pallas_call(
        functools.partial(update_kernel, step_scale, rank),
        out_shape=jax.ShapeDtypeStruct((width, 2, local_units), f32),
        grid=(blocks, width // block),
        in_specs=[
            pl.BlockSpec((width, rank * members), lambda j, i: (0, 0)),
            pl.BlockSpec((1, rank * members, 2 * LANES), lambda j, i: (j, 0, 0)),
            pl.BlockSpec((members, LANES), lambda j, i: (0, 0)),
        ],
        out_specs=pl.BlockSpec((block, 2, LANES), lambda j, i: (i, 0, j)),
        scratch_shapes=[pltpu.VMEM((rank * members, 2 * LANES), bf16)],
        compiler_params=pltpu.CompilerParams(vmem_limit_bytes=VMEM_LIMIT),
        name="update",
    )(full_factor.reshape(width, rank * members), noise, all_fitness)
    return outputs, fitness[:, 0], update


def body(n, members_in, gate_up, down_weight, factor_in, factor_out, target):
    own_rows, width = members_in.shape
    local_units = gate_up.shape[2]
    members, rank, local_width = factor_in.shape
    aligned = local_units % LANES == 0 and local_width % LANES == 0 and members == LANES
    if aligned and n % 4 == 0 and n > 4 and own_rows == 8 and rank <= 8:
        return fast_body(n, members_in, gate_up, down_weight, factor_in, factor_out, target)
    return plain_body(members_in, gate_up, down_weight, factor_in, factor_out, target)


def plain_body(members_in, gate_up, down_weight, factor_in, factor_out, target):
    own_rows = members_in.shape[0]
    width = gate_up.shape[0]
    local_units = gate_up.shape[2]
    members = factor_in.shape[0]
    rank = factor_in.shape[1]
    whole_x = lax.all_gather(members_in, "row", axis=0, tiled=True)
    full_factor = lax.all_gather(factor_in, "row", axis=2, tiled=True)
    projected = jnp.einsum("md,mrd->mr", whole_x, full_factor, preferred_element_type=jnp.float32)
    stacked = jnp.dot(
        whole_x, gate_up.reshape(width, 2 * local_units), preferred_element_type=jnp.float32
    )
    stacked = stacked.reshape(members, 2, local_units)
    noise = jnp.sum(projected[:, :, None, None] * factor_out, axis=1)
    stacked = stacked + noise * (noise_scale / math.sqrt(rank))
    hidden = (jax.nn.silu(stacked[:, 0]) * stacked[:, 1]).astype(jnp.bfloat16)
    sums = lax.psum_scatter(
        jnp.dot(hidden, down_weight, preferred_element_type=jnp.float32),
        "row",
        scatter_dimension=0,
        tiled=True,
    )
    own_losses = jnp.mean((sums - target) ** 2, axis=1)
    losses = lax.all_gather(own_losses, "row", axis=0, tiled=True)
    average = jnp.mean(losses)
    spread = jnp.mean((losses - average) ** 2)
    all_fitness = (average - losses) / jnp.sqrt(spread + 1e-06)
    own_fitness = lax.dynamic_slice_in_dim(
        all_fitness, lax.axis_index("row") * own_rows, own_rows, 0
    )
    scaled = (all_fitness[:, None, None, None] * factor_out).astype(jnp.bfloat16)
    step_scale = math.sqrt(width / (members * rank))
    contract = (((0, 1), (0, 1)), ((), ()))
    update = lax.dot_general(full_factor, scaled, contract, preferred_element_type=jnp.float32)
    update = update * step_scale
    return (sums.astype(jnp.bfloat16), own_fitness, update)


def solution(mesh):
    return jax.shard_map(
        functools.partial(body, mesh.shape["row"]),
        mesh=mesh,
        in_specs=(
            P(("grp", "row"), None),
            P(None, None, "row"),
            P("row", None),
            P("grp", None, "row"),
            P("grp", None, None, "row"),
            P(("grp", "row"), None),
        ),
        out_specs=(P(("grp", "row"), None), P(("grp", "row")), P("grp", None, "row")),
        check_vma=False,
    )
```

```python
import functools
import math

import jax
import jax.numpy as jnp
from jax import lax
from jax.experimental import pallas as pl
from jax.experimental.pallas import tpu as pltpu
from jax.sharding import PartitionSpec as P

noise_scale = 0.5
MESH = pl.DeviceIdType.MESH
LANES = 128
VMEM_LIMIT = 62 * 1024 * 1024


class Gather:
    def __init__(self, depth, place, own, slots, send_sems, recv_sems, local_sem):
        self.depth, self.place = depth, place
        self.own, self.slots = own, slots
        self.send_sems, self.recv_sems, self.local_sem = send_sems, recv_sems, local_sem
        self.sent = []

    def index(self, z, y, c):
        return (z * 2 + y) * 2 + c

    def copy(self, source, origin, target):
        sem = self.send_sems.at[len(self.sent)]
        return pltpu.make_async_remote_copy(
            src_ref=source,
            dst_ref=self.slots.at[origin],
            send_sem=sem,
            recv_sem=self.recv_sems.at[origin],
            device_id={"row": target},
            device_id_type=MESH,
        )

    def send(self, source, origin, target, condition):
        copy = self.copy(source, origin, target)
        self.sent.append((condition, copy))
        if condition is None:
            copy.start()
        else:
            pl.when(condition)(copy.start)

    def arrive(self, origin, condition):
        z, y, c = self.place
        copy = pltpu.make_async_remote_copy(
            src_ref=self.slots.at[origin],
            dst_ref=self.slots.at[origin],
            send_sem=self.send_sems.at[0],
            recv_sem=self.recv_sems.at[origin],
            device_id={"row": self.index(z, y, 1 - c)},
            device_id_type=MESH,
        )
        if condition is None:
            copy.wait_recv()
        else:
            pl.when(condition)(copy.wait_recv)

    def start(self):
        z, y, c = self.place
        me = self.index(z, y, c)
        self.local = pltpu.make_async_copy(self.own, self.slots.at[me], self.local_sem)
        self.local.start()
        up, down = z + 1 < self.depth, z >= 1
        self.send(self.own, me, self.index(jnp.minimum(z + 1, self.depth - 1), y, c), up)
        self.send(self.own, me, self.index(jnp.maximum(z - 1, 0), y, c), down)

    def start_rest(self):
        z, y, c = self.place
        me = self.index(z, y, c)
        self.send(self.own, me, self.index(z, 1 - y, c), None)
        self.send(self.own, me, self.index(z, y, 1 - c), None)

    def along_z(self, step):
        z, y, c = self.place
        for sign in (-1, 1):
            at = z + sign * (1 + step)
            here = (at >= 0) & (at < self.depth)
            origin = self.index(jnp.clip(at, 0, self.depth - 1), y, c)
            self.arrive(origin, here)
            on = z - sign
            further = here & (on >= 0) & (on < self.depth)
            source = self.slots.at[origin]
            if step < self.depth - 2:
                self.send(
                    source, origin, self.index(jnp.clip(on, 0, self.depth - 1), y, c), further
                )
            self.send(source, origin, self.index(z, 1 - y, c), here)
            self.send(source, origin, self.index(z, y, 1 - c), here)

    def along_y(self, step):
        z, y, c = self.place
        for sign in (-1, 1) if step else (1,):
            at = z + sign * step
            here = (at >= 0) & (at < self.depth) if step else None
            origin = self.index(jnp.clip(at, 0, self.depth - 1), 1 - y, c)
            self.arrive(origin, here)
            self.send(self.slots.at[origin], origin, self.index(z, y, 1 - c), here)

    def finish(self):
        z, y, c = self.place
        for at in range(self.depth):
            for side in range(2):
                self.arrive(self.index(at, side, 1 - c), None)
        self.local.wait()

    def drain(self):
        for condition, copy in self.sent:
            if condition is None:
                copy.wait_send()
            else:
                pl.when(condition)(copy.wait_send)


def sends_of(depth):
    return 4 + 6 * (depth - 1) + 2 * depth


def forward_kernel(
    n, rank, chunks, lag,
    x_ref, factor_ref, target_ref, gate_up_ref, down_ref, out_factor_ref,
    outputs_ref, fitness_ref, all_fitness_ref, full_factor_ref, noise_ref,
    weights, down, raw, wide, x_all, x_mixed, acc, hidden, proj_in, proj_out, loss_in, loss_out,
    pair_out, pair_keep, pair_in, y_out, y_keep, y_in, z_out, z_keep, z_in, sums,
    weight_sems, down_sem, raw_sems, local_sems,
    x_send, x_recv, f_send, f_recv, p_send, p_recv, l_send, l_recv,
    c_send, c_recv, y_send, y_recv, z_send, z_recv,
):
    depth = n // 4
    me = lax.axis_index("row")
    c = lax.rem(me, 2)
    y = lax.rem(me // 2, 2)
    z = me // 4
    own_rows, width = x_ref.shape
    members = n * own_rows
    local_width = factor_ref.shape[0]
    blocks = weights.shape[0]

    loads = []
    for j in range(blocks):
        cut = pl.ds(j * LANES, LANES)
        raw_copy = pltpu.make_async_copy(out_factor_ref.at[:, :, cut], raw.at[j], raw_sems.at[j])
        raw_copy.start()
        loads.append(raw_copy)
    weight_loads = []
    for j in range(blocks):
        cut = pl.ds(j * LANES, LANES)
        copy = pltpu.make_async_copy(gate_up_ref.at[:, :, cut], weights.at[j], weight_sems.at[j])
        copy.start()
        weight_loads.append(copy)
    down_load = pltpu.make_async_copy(down_ref, down, down_sem)
    down_load.start()

    barrier = pltpu.get_barrier_semaphore()
    for k in range(1, n):
        pl.semaphore_signal(
            barrier, inc=1, device_id={"row": lax.rem(me + k, n)}, device_id_type=MESH
        )
    pl.semaphore_wait(barrier, n - 1)

    x_gather = Gather(depth, (z, y, c), x_ref, x_all, x_send, x_recv, local_sems.at[0])
    f_gather = Gather(
        depth, (z, y, c), factor_ref, full_factor_ref, f_send, f_recv, local_sems.at[1]
    )
    x_gather.start()
    x_gather.start_rest()

    def split(j):
        loads[j].wait()
        wide[...] = raw.at[j].reshape(members * rank * 2, LANES)[...].astype(jnp.float32)
        for r in range(rank):
            for k in range(2):
                part = wide[pl.ds(r * 2 + k, members, 2 * rank), :]
                noise_ref[j, r * members:(r + 1) * members, k * LANES:(k + 1) * LANES] = (
                    part.astype(jnp.bfloat16)
                )

    for step in range(depth - 1):
        x_gather.along_z(step)
        x_gather.along_y(step)
        split(step)
    f_gather.start()
    x_gather.along_y(depth - 1)
    x_gather.finish()
    f_gather.start_rest()

    def to_all(source, slots, send_sems, recv_sems):
        copies = []
        for k in range(1, n):
            copy = pltpu.make_async_remote_copy(
                src_ref=source,
                dst_ref=slots.at[k],
                send_sem=send_sems.at[k],
                recv_sem=recv_sems.at[k],
                device_id={"row": lax.rem(me + k, n)},
                device_id_type=MESH,
            )
            copy.start()
            copies.append(copy)
        return copies

    own_columns = pl.ds(pl.multiple_of(me * local_width, LANES), local_width)
    x_own = x_all[:, :, own_columns].reshape(members, local_width)
    crossed = jnp.dot(x_own, factor_ref[...], preferred_element_type=jnp.float32)
    row_at = lax.broadcasted_iota(jnp.int32, (members, members), 0)
    lane_at = lax.broadcasted_iota(jnp.int32, (members, members), 1)
    proj_out[...] = jnp.zeros_like(proj_out)
    for r in range(rank):
        block = crossed[:, r * members:(r + 1) * members]
        proj_out[r:r + 1, :] = jnp.sum(
            jnp.where(row_at == lane_at, block, 0.0), axis=0, keepdims=True
        )
    proj_copies = to_all(proj_out, proj_in, p_send, p_recv)

    spread_row = lax.broadcasted_iota(jnp.int32, (LANES, 2 * LANES), 0)
    spread_lane = lax.broadcasted_iota(jnp.int32, (LANES, 2 * LANES), 1)
    to_gate = jnp.where(spread_lane == 2 * spread_row, 1.0, 0.0).astype(jnp.bfloat16)
    to_up = jnp.where(spread_lane == 2 * spread_row + 1, 1.0, 0.0).astype(jnp.bfloat16)

    @pl.loop(0, width // LANES, unroll=4)
    def _(i):
        piece = x_all[:, :, pl.ds(pl.multiple_of(i * LANES, LANES), LANES)]
        piece = piece.reshape(members, LANES)
        cut = pl.ds(pl.multiple_of(i * 2 * LANES, LANES), 2 * LANES)
        x_mixed[0:members, cut] = jnp.dot(
            piece, to_gate, preferred_element_type=jnp.float32
        ).astype(jnp.bfloat16)
        x_mixed[members:2 * members, cut] = jnp.dot(
            piece, to_up, preferred_element_type=jnp.float32
        ).astype(jnp.bfloat16)

    for j in range(depth - 1, blocks):
        split(j)

    deep = 2 * width // 4
    for first in range(0, blocks, 2):
        group = list(range(first, min(first + 2, blocks)))
        for j in group:
            weight_loads[j].wait()
        views = [weights.at[j].reshape(2 * width, LANES) for j in group]
        lanes = slice(first * LANES, (first + len(group)) * LANES)

        def piece(i):
            rows = pl.ds(pl.multiple_of(i * deep, LANES), deep)
            w = [view[rows, :] for view in views]
            w = jnp.concatenate(w, axis=1) if len(w) > 1 else w[0]
            return jnp.dot(x_mixed[:, rows], w, preferred_element_type=jnp.float32)

        acc[:, lanes] = piece(0)

        @pl.loop(1, 2 * width // deep)
        def _(i):
            acc[:, lanes] += piece(i)

        if first == 2:
            f_gather.along_z(0)
            f_gather.along_y(0)

    for copy in proj_copies:
        copy.wait()
    projected = proj_out[...]
    for k in range(1, n):
        projected = projected + proj_in[k]
    columns = [
        jnp.sum(
            jnp.where(row_at == lane_at, projected[r:r + 1, :], 0.0), axis=1, keepdims=True
        )
        for r in range(rank)
    ]

    for j in range(blocks):
        lanes = slice(j * LANES, (j + 1) * LANES)
        two = []
        for k in range(2):
            noise = jnp.zeros((members, LANES), jnp.float32)
            for r in range(rank):
                noise += columns[r] * noise_ref[
                    j, r * members:(r + 1) * members, k * LANES:(k + 1) * LANES
                ].astype(jnp.float32)
            two.append(
                acc[k * members:(k + 1) * members, lanes]
                + noise * (noise_scale / math.sqrt(rank))
            )
        hidden[:, j * LANES:(j + 1) * LANES] = (
            (two[0] / (1.0 + jnp.exp(-two[0]))) * two[1]
        ).astype(jnp.bfloat16)

    f_gather.along_z(1)
    f_gather.along_y(1)
    down_load.wait()

    span = width // chunks
    sibling, across = (z * 2 + y) * 2 + 1 - c, (z * 2 + 1 - y) * 2 + c
    pair_copies, y_copies, z_copies = [], [], []

    def down_step(i):
        part = jnp.dot(
            hidden[...], down[:, i * span:(i + 1) * span], preferred_element_type=jnp.float32
        ).reshape(2 * depth, 2, own_rows, span)
        first, second = part[:, 0], part[:, 1]
        pair_keep[i] = jnp.where(c == 0, first, second)
        pair_out[i] = jnp.where(c == 0, second, first)
        copy = pltpu.make_async_remote_copy(
            src_ref=pair_out.at[i], dst_ref=pair_in.at[i],
            send_sem=c_send.at[i], recv_sem=c_recv.at[i],
            device_id={"row": sibling}, device_id_type=MESH,
        )
        copy.start()
        pair_copies.append(copy)

    def y_step(i):
        pair_copies[i].wait_recv()
        part = (pair_keep[i] + pair_in[i]).reshape(depth, 2, own_rows, span)
        first, second = part[:, 0], part[:, 1]
        y_keep[i] = jnp.where(y == 0, first, second)
        y_out[i] = (
            jnp.where(y == 0, second, first).reshape(depth * own_rows, span).astype(jnp.bfloat16)
        )
        copy = pltpu.make_async_remote_copy(
            src_ref=y_out.at[i], dst_ref=y_in.at[i],
            send_sem=y_send.at[i], recv_sem=y_recv.at[i],
            device_id={"row": across}, device_id_type=MESH,
        )
        copy.start()
        y_copies.append(copy)

    def z_step(i):
        y_copies[i].wait_recv()
        part = y_keep[i] + y_in[i].astype(jnp.float32).reshape(depth, own_rows, span)
        z_keep[i] = part
        z_out[i] = part.astype(jnp.bfloat16)
        copies = []
        for k in range(1, depth):
            to = lax.rem(z + k, depth)
            copy = pltpu.make_async_remote_copy(
                src_ref=z_out.at[i, to], dst_ref=z_in.at[i, k],
                send_sem=z_send.at[i, k], recv_sem=z_recv.at[i, k],
                device_id={"row": (to * 2 + y) * 2 + c}, device_id_type=MESH,
            )
            copy.start()
            copies.append(copy)
        z_copies.append(copies)

    for t in range(chunks + 2 * lag):
        if t < chunks:
            down_step(t)
        if 0 <= t - lag < chunks:
            y_step(t - lag)
        if 0 <= t - 2 * lag < chunks:
            z_step(t - 2 * lag)
        if t == chunks + lag - 1:
            for step in range(2, depth - 1):
                f_gather.along_z(step)
                f_gather.along_y(step)

    total = jnp.zeros((own_rows, 1), jnp.float32)
    for i in range(chunks):
        part = z_keep[i, z]
        for k in range(1, depth):
            z_copies[i][k - 1].wait_recv()
            part = part + z_in[i, k].astype(jnp.float32)
        cut = slice(i * span, (i + 1) * span)
        outputs_ref[:, cut] = part.astype(jnp.bfloat16)
        miss = part - target_ref[:, cut]
        total = total + jnp.sum(miss * miss, axis=1, keepdims=True)
    loss_out[...] = jnp.broadcast_to(total / width, loss_out.shape)
    loss_copies = to_all(loss_out, loss_in, l_send, l_recv)
    f_gather.along_y(depth - 1)
    for copy in loss_copies:
        copy.wait()
    loss_in[0] = loss_out[...]

    def by_member(slot):
        return loss_in[slot]

    average = jnp.zeros((1, LANES), jnp.float32)
    for k in range(n):
        average = average + jnp.sum(loss_in[k], axis=0, keepdims=True)
    average = average / members
    spread = jnp.zeros((1, LANES), jnp.float32)
    for k in range(n):
        away = loss_in[k] - average
        spread = spread + jnp.sum(away * away, axis=0, keepdims=True)
    scale = jnp.sqrt(spread / members + 1e-06)
    for d in range(n):
        slot = lax.rem(me - d + n, n)
        all_fitness_ref[d * own_rows:(d + 1) * own_rows, :] = (
            average - loss_in[slot]
        ) / scale
    fitness_ref[...] = (average - loss_in[0]) / scale

    f_gather.finish()
    x_gather.drain()
    f_gather.drain()
    for copy in pair_copies + y_copies + [copy for some in z_copies for copy in some]:
        copy.wait_send()


def update_kernel(scale, rank, factor_ref, noise_ref, fitness_ref, update_ref, scaled):
    members = fitness_ref.shape[0]
    rows = update_ref.shape[0]

    @pl.when(pl.program_id(1) == 0)
    def _():
        fitness = fitness_ref[...]
        for r in range(rank):
            for k in range(2):
                at = (slice(r * members, (r + 1) * members), slice(k * LANES, (k + 1) * LANES))
                scaled[at] = (
                    fitness * noise_ref[(0,) + at].astype(jnp.float32)
                ).astype(jnp.bfloat16)

    start = pl.multiple_of(pl.program_id(1) * rows, LANES)
    result = jnp.dot(
        factor_ref[pl.ds(start, rows), :], scaled[...], preferred_element_type=jnp.float32
    ) * scale
    view = update_ref.reshape(2 * rows, LANES)
    view[pl.ds(0, rows, 2), :] = result[:, :LANES]
    view[pl.ds(1, rows, 2), :] = result[:, LANES:]


def fast_body(n, members_in, gate_up, down_weight, factor_in, factor_out, target):
    own_rows, width = members_in.shape
    local_units = gate_up.shape[2]
    members, rank, local_width = factor_in.shape
    blocks = local_units // LANES
    depth = n // 4
    chunks, lag = 8, 2
    span = width // chunks
    factor = factor_in.transpose(2, 1, 0).reshape(local_width, rank * members)
    rows_out = factor_out.reshape(members * rank, 2, local_units)
    bf16, f32 = jnp.bfloat16, jnp.float32
    dma = pltpu.SemaphoreType.DMA
    vmem = pl.BlockSpec(memory_space=pltpu.VMEM)
    hbm = pl.BlockSpec(memory_space=pl.ANY)
    outputs, fitness, all_fitness, full_factor, noise = pl.pallas_call(
        functools.partial(forward_kernel, n, rank, chunks, lag),
        out_shape=(
            jax.ShapeDtypeStruct((own_rows, width), bf16),
            jax.ShapeDtypeStruct((own_rows, LANES), f32),
            jax.ShapeDtypeStruct((members, LANES), f32),
            jax.ShapeDtypeStruct((n, local_width, rank * members), bf16),
            jax.ShapeDtypeStruct((blocks, rank * members, 2 * LANES), bf16),
        ),
        in_specs=[vmem, vmem, vmem, hbm, hbm, hbm],
        out_specs=(vmem, vmem, vmem, hbm, vmem),
        scratch_shapes=[
            pltpu.VMEM((blocks, width, 2, LANES), bf16),
            pltpu.VMEM((local_units, width), bf16),
            pltpu.VMEM((blocks, members * rank, 2, LANES), bf16),
            pltpu.VMEM((members * rank * 2, LANES), f32),
            pltpu.VMEM((n, own_rows, width), bf16),
            pltpu.VMEM((2 * members, 2 * width), bf16),
            pltpu.VMEM((2 * members, local_units), f32),
            pltpu.VMEM((members, local_units), bf16),
            pltpu.VMEM((n, 8, members), f32),
            pltpu.VMEM((8, members), f32),
            pltpu.VMEM((n, own_rows, LANES), f32),
            pltpu.VMEM((own_rows, LANES), f32),
            pltpu.VMEM((chunks, 2 * depth, own_rows, span), f32),
            pltpu.VMEM((chunks, 2 * depth, own_rows, span), f32),
            pltpu.VMEM((chunks, 2 * depth, own_rows, span), f32),
            pltpu.VMEM((chunks, depth * own_rows, span), bf16),
            pltpu.VMEM((chunks, depth, own_rows, span), f32),
            pltpu.VMEM((chunks, depth * own_rows, span), bf16),
            pltpu.VMEM((chunks, depth, own_rows, span), bf16),
            pltpu.VMEM((chunks, depth, own_rows, span), f32),
            pltpu.VMEM((chunks, depth, own_rows, span), bf16),
            pltpu.VMEM((8, LANES), f32),
            dma((blocks,)), dma(()), dma((blocks,)), dma((2,)),
            dma((sends_of(depth),)), dma((n,)),
            dma((sends_of(depth),)), dma((n,)),
            dma((n,)), dma((n,)), dma((n,)), dma((n,)),
            dma((chunks,)), dma((chunks,)), dma((chunks,)), dma((chunks,)),
            dma((chunks, depth)), dma((chunks, depth)),
        ],
        compiler_params=pltpu.CompilerParams(
            collective_id=0, has_side_effects=True, vmem_limit_bytes=VMEM_LIMIT
        ),
        name="forward",
    )(members_in, factor, target, gate_up, down_weight, rows_out)

    block = width
    step_scale = math.sqrt(width / (members * rank))
    update = pl.pallas_call(
        functools.partial(update_kernel, step_scale, rank),
        out_shape=jax.ShapeDtypeStruct((width, 2, local_units), f32),
        grid=(blocks, width // block),
        in_specs=[
            pl.BlockSpec((width, rank * members), lambda j, i: (0, 0)),
            pl.BlockSpec((1, rank * members, 2 * LANES), lambda j, i: (j, 0, 0)),
            pl.BlockSpec((members, LANES), lambda j, i: (0, 0)),
        ],
        out_specs=pl.BlockSpec((block, 2, LANES), lambda j, i: (i, 0, j)),
        scratch_shapes=[pltpu.VMEM((rank * members, 2 * LANES), bf16)],
        compiler_params=pltpu.CompilerParams(vmem_limit_bytes=VMEM_LIMIT),
        name="update",
    )(full_factor.reshape(width, rank * members), noise, all_fitness)
    return outputs, fitness[:, 0], update


def body(n, members_in, gate_up, down_weight, factor_in, factor_out, target):
    own_rows, width = members_in.shape
    local_units = gate_up.shape[2]
    members, rank, local_width = factor_in.shape
    aligned = local_units % LANES == 0 and local_width % LANES == 0 and members == LANES
    if aligned and n % 4 == 0 and n > 4 and own_rows == 8 and rank <= 8:
        return fast_body(n, members_in, gate_up, down_weight, factor_in, factor_out, target)
    return plain_body(members_in, gate_up, down_weight, factor_in, factor_out, target)


def plain_body(members_in, gate_up, down_weight, factor_in, factor_out, target):
    own_rows = members_in.shape[0]
    width = gate_up.shape[0]
    local_units = gate_up.shape[2]
    members = factor_in.shape[0]
    rank = factor_in.shape[1]
    whole_x = lax.all_gather(members_in, "row", axis=0, tiled=True)
    full_factor = lax.all_gather(factor_in, "row", axis=2, tiled=True)
    projected = jnp.einsum("md,mrd->mr", whole_x, full_factor, preferred_element_type=jnp.float32)
    stacked = jnp.dot(
        whole_x, gate_up.reshape(width, 2 * local_units), preferred_element_type=jnp.float32
    )
    stacked = stacked.reshape(members, 2, local_units)
    noise = jnp.sum(projected[:, :, None, None] * factor_out, axis=1)
    stacked = stacked + noise * (noise_scale / math.sqrt(rank))
    hidden = (jax.nn.silu(stacked[:, 0]) * stacked[:, 1]).astype(jnp.bfloat16)
    sums = lax.psum_scatter(
        jnp.dot(hidden, down_weight, preferred_element_type=jnp.float32),
        "row",
        scatter_dimension=0,
        tiled=True,
    )
    own_losses = jnp.mean((sums - target) ** 2, axis=1)
    losses = lax.all_gather(own_losses, "row", axis=0, tiled=True)
    average = jnp.mean(losses)
    spread = jnp.mean((losses - average) ** 2)
    all_fitness = (average - losses) / jnp.sqrt(spread + 1e-06)
    own_fitness = lax.dynamic_slice_in_dim(
        all_fitness, lax.axis_index("row") * own_rows, own_rows, 0
    )
    scaled = (all_fitness[:, None, None, None] * factor_out).astype(jnp.bfloat16)
    step_scale = math.sqrt(width / (members * rank))
    contract = (((0, 1), (0, 1)), ((), ()))
    update = lax.dot_general(full_factor, scaled, contract, preferred_element_type=jnp.float32)
    update = update * step_scale
    return (sums.astype(jnp.bfloat16), own_fitness, update)


def solution(mesh):
    return jax.shard_map(
        functools.partial(body, mesh.shape["row"]),
        mesh=mesh,
        in_specs=(
            P(("grp", "row"), None),
            P(None, None, "row"),
            P("row", None),
            P("grp", None, "row"),
            P("grp", None, None, "row"),
            P(("grp", "row"), None),
        ),
        out_specs=(P(("grp", "row"), None), P(("grp", "row")), P("grp", None, "row")),
        check_vma=False,
    )
```

```python
import functools
import math

import jax
import jax.numpy as jnp
from jax import lax
from jax.experimental import pallas as pl
from jax.experimental.pallas import tpu as pltpu
from jax.sharding import PartitionSpec as P

noise_scale = 0.5
MESH = pl.DeviceIdType.MESH
LANES = 128
VMEM_LIMIT = 62 * 1024 * 1024


class Gather:
    def __init__(self, depth, place, own, slots, send_sems, recv_sems, local_sem, direct):
        self.direct = direct
        self.depth, self.place = depth, place
        self.own, self.slots = own, slots
        self.send_sems, self.recv_sems, self.local_sem = send_sems, recv_sems, local_sem
        self.sent = []

    def index(self, z, y, c):
        return (z * 2 + y) * 2 + c

    def copy(self, source, origin, target):
        sem = self.send_sems.at[len(self.sent)]
        return pltpu.make_async_remote_copy(
            src_ref=source,
            dst_ref=self.slots.at[origin],
            send_sem=sem,
            recv_sem=self.recv_sems.at[origin],
            device_id={"row": target},
            device_id_type=MESH,
        )

    def send(self, source, origin, target, condition):
        copy = self.copy(source, origin, target)
        self.sent.append((condition, copy))
        if condition is None:
            copy.start()
        else:
            pl.when(condition)(copy.start)

    def arrive(self, origin, condition):
        z, y, c = self.place
        copy = pltpu.make_async_remote_copy(
            src_ref=self.slots.at[origin],
            dst_ref=self.slots.at[origin],
            send_sem=self.send_sems.at[0],
            recv_sem=self.recv_sems.at[origin],
            device_id={"row": self.index(z, y, 1 - c)},
            device_id_type=MESH,
        )
        if condition is None:
            copy.wait_recv()
        else:
            pl.when(condition)(copy.wait_recv)

    def start(self):
        z, y, c = self.place
        me = self.index(z, y, c)
        self.local = pltpu.make_async_copy(self.own, self.slots.at[me], self.local_sem)
        self.local.start()
        for hop in range(1, self.depth if self.direct else 2):
            for to in (z + hop, z - hop):
                there = (to >= 0) & (to < self.depth)
                target = self.index(jnp.clip(to, 0, self.depth - 1), y, c)
                self.send(self.own, me, target, there)

    def start_rest(self):
        z, y, c = self.place
        me = self.index(z, y, c)
        self.send(self.own, me, self.index(z, 1 - y, c), None)
        self.send(self.own, me, self.index(z, y, 1 - c), None)

    def along_z(self, step):
        z, y, c = self.place
        for sign in (-1, 1):
            at = z + sign * (1 + step)
            here = (at >= 0) & (at < self.depth)
            origin = self.index(jnp.clip(at, 0, self.depth - 1), y, c)
            self.arrive(origin, here)
            on = z - sign
            further = here & (on >= 0) & (on < self.depth)
            source = self.slots.at[origin]
            if step < self.depth - 2 and not self.direct:
                self.send(
                    source, origin, self.index(jnp.clip(on, 0, self.depth - 1), y, c), further
                )
            self.send(source, origin, self.index(z, 1 - y, c), here)
            self.send(source, origin, self.index(z, y, 1 - c), here)

    def along_y(self, step):
        z, y, c = self.place
        for sign in (-1, 1) if step else (1,):
            at = z + sign * step
            here = (at >= 0) & (at < self.depth) if step else None
            origin = self.index(jnp.clip(at, 0, self.depth - 1), 1 - y, c)
            self.arrive(origin, here)
            self.send(self.slots.at[origin], origin, self.index(z, y, 1 - c), here)

    def finish(self):
        z, y, c = self.place
        for at in range(self.depth):
            for side in range(2):
                self.arrive(self.index(at, side, 1 - c), None)
        self.local.wait()

    def drain(self):
        for condition, copy in self.sent:
            if condition is None:
                copy.wait_send()
            else:
                pl.when(condition)(copy.wait_send)


def sends_of(depth):
    return 4 + 6 * (depth - 1) + 2 * depth


def forward_kernel(
    n, rank, chunks, lag,
    x_ref, factor_ref, target_ref, gate_up_ref, down_ref, out_factor_ref,
    outputs_ref, fitness_ref, all_fitness_ref, full_factor_ref, noise_ref,
    weights, down, raw, wide, x_all, x_mixed, acc, hidden, proj_in, proj_out, loss_in, loss_out,
    pair_out, pair_keep, pair_in, y_out, y_keep, y_in, z_out, z_keep, z_in, sums,
    weight_sems, down_sem, raw_sems, local_sems,
    x_send, x_recv, f_send, f_recv, p_send, p_recv, l_send, l_recv,
    c_send, c_recv, y_send, y_recv, z_send, z_recv,
):
    depth = n // 4
    me = lax.axis_index("row")
    c = lax.rem(me, 2)
    y = lax.rem(me // 2, 2)
    z = me // 4
    own_rows, width = x_ref.shape
    members = n * own_rows
    local_width = factor_ref.shape[0]
    blocks = weights.shape[0]

    loads = []
    for j in range(blocks):
        cut = pl.ds(j * LANES, LANES)
        raw_copy = pltpu.make_async_copy(out_factor_ref.at[:, :, cut], raw.at[j], raw_sems.at[j])
        raw_copy.start()
        loads.append(raw_copy)
    weight_loads = []
    for j in range(blocks):
        cut = pl.ds(j * LANES, LANES)
        copy = pltpu.make_async_copy(gate_up_ref.at[:, :, cut], weights.at[j], weight_sems.at[j])
        copy.start()
        weight_loads.append(copy)
    down_load = pltpu.make_async_copy(down_ref, down, down_sem)
    down_load.start()

    barrier = pltpu.get_barrier_semaphore()
    for k in range(1, n):
        pl.semaphore_signal(
            barrier, inc=1, device_id={"row": lax.rem(me + k, n)}, device_id_type=MESH
        )
    pl.semaphore_wait(barrier, n - 1)

    x_gather = Gather(
        depth, (z, y, c), x_ref, x_all, x_send, x_recv, local_sems.at[0], True
    )
    f_gather = Gather(
        depth, (z, y, c), factor_ref, full_factor_ref, f_send, f_recv, local_sems.at[1], False
    )
    x_gather.start()
    x_gather.start_rest()

    def split(j):
        loads[j].wait()
        wide[...] = raw.at[j].reshape(members * rank * 2, LANES)[...].astype(jnp.float32)
        for r in range(rank):
            for k in range(2):
                part = wide[pl.ds(r * 2 + k, members, 2 * rank), :]
                noise_ref[j, r * members:(r + 1) * members, k * LANES:(k + 1) * LANES] = (
                    part.astype(jnp.bfloat16)
                )

    for step in range(depth - 1):
        split(step)
    for step in range(depth - 1):
        x_gather.along_z(step)
        x_gather.along_y(step)
    f_gather.start()
    x_gather.along_y(depth - 1)
    x_gather.finish()
    f_gather.start_rest()

    def to_all(source, slots, send_sems, recv_sems):
        copies = []
        for k in range(1, n):
            copy = pltpu.make_async_remote_copy(
                src_ref=source,
                dst_ref=slots.at[k],
                send_sem=send_sems.at[k],
                recv_sem=recv_sems.at[k],
                device_id={"row": lax.rem(me + k, n)},
                device_id_type=MESH,
            )
            copy.start()
            copies.append(copy)
        return copies

    own_columns = pl.ds(pl.multiple_of(me * local_width, LANES), local_width)
    x_own = x_all[:, :, own_columns].reshape(members, local_width)
    crossed = jnp.dot(x_own, factor_ref[...], preferred_element_type=jnp.float32)
    row_at = lax.broadcasted_iota(jnp.int32, (members, members), 0)
    lane_at = lax.broadcasted_iota(jnp.int32, (members, members), 1)
    proj_out[...] = jnp.zeros_like(proj_out)
    for r in range(rank):
        block = crossed[:, r * members:(r + 1) * members]
        proj_out[r:r + 1, :] = jnp.sum(
            jnp.where(row_at == lane_at, block, 0.0), axis=0, keepdims=True
        )
    proj_copies = to_all(proj_out, proj_in, p_send, p_recv)

    spread_row = lax.broadcasted_iota(jnp.int32, (LANES, 2 * LANES), 0)
    spread_lane = lax.broadcasted_iota(jnp.int32, (LANES, 2 * LANES), 1)
    to_gate = jnp.where(spread_lane == 2 * spread_row, 1.0, 0.0).astype(jnp.bfloat16)
    to_up = jnp.where(spread_lane == 2 * spread_row + 1, 1.0, 0.0).astype(jnp.bfloat16)

    @pl.loop(0, width // LANES, unroll=4)
    def _(i):
        piece = x_all[:, :, pl.ds(pl.multiple_of(i * LANES, LANES), LANES)]
        piece = piece.reshape(members, LANES)
        cut = pl.ds(pl.multiple_of(i * 2 * LANES, LANES), 2 * LANES)
        x_mixed[0:members, cut] = jnp.dot(
            piece, to_gate, preferred_element_type=jnp.float32
        ).astype(jnp.bfloat16)
        x_mixed[members:2 * members, cut] = jnp.dot(
            piece, to_up, preferred_element_type=jnp.float32
        ).astype(jnp.bfloat16)

    for j in range(depth - 1, blocks):
        split(j)

    deep = 2 * width // 4
    for first in range(0, blocks, 2):
        group = list(range(first, min(first + 2, blocks)))
        for j in group:
            weight_loads[j].wait()
        views = [weights.at[j].reshape(2 * width, LANES) for j in group]
        lanes = slice(first * LANES, (first + len(group)) * LANES)

        def piece(i):
            rows = pl.ds(pl.multiple_of(i * deep, LANES), deep)
            w = [view[rows, :] for view in views]
            w = jnp.concatenate(w, axis=1) if len(w) > 1 else w[0]
            return jnp.dot(x_mixed[:, rows], w, preferred_element_type=jnp.float32)

        acc[:, lanes] = piece(0)

        @pl.loop(1, 2 * width // deep)
        def _(i):
            acc[:, lanes] += piece(i)

        if first == 2:
            f_gather.along_z(0)
            f_gather.along_y(0)

    for copy in proj_copies:
        copy.wait()
    projected = proj_out[...]
    for k in range(1, n):
        projected = projected + proj_in[k]
    columns = [
        jnp.sum(
            jnp.where(row_at == lane_at, projected[r:r + 1, :], 0.0), axis=1, keepdims=True
        )
        for r in range(rank)
    ]

    for j in range(blocks):
        lanes = slice(j * LANES, (j + 1) * LANES)
        two = []
        for k in range(2):
            noise = jnp.zeros((members, LANES), jnp.float32)
            for r in range(rank):
                noise += columns[r] * noise_ref[
                    j, r * members:(r + 1) * members, k * LANES:(k + 1) * LANES
                ].astype(jnp.float32)
            two.append(
                acc[k * members:(k + 1) * members, lanes]
                + noise * (noise_scale / math.sqrt(rank))
            )
        hidden[:, j * LANES:(j + 1) * LANES] = (
            (two[0] / (1.0 + jnp.exp(-two[0]))) * two[1]
        ).astype(jnp.bfloat16)

    f_gather.along_z(1)
    f_gather.along_y(1)
    down_load.wait()

    span = width // chunks
    sibling, across = (z * 2 + y) * 2 + 1 - c, (z * 2 + 1 - y) * 2 + c
    pair_copies, y_copies, z_copies = [], [], []

    def down_step(i):
        part = jnp.dot(
            hidden[...], down[:, i * span:(i + 1) * span], preferred_element_type=jnp.float32
        ).reshape(2 * depth, 2, own_rows, span)
        first, second = part[:, 0], part[:, 1]
        pair_keep[i] = jnp.where(c == 0, first, second)
        pair_out[i] = jnp.where(c == 0, second, first)
        copy = pltpu.make_async_remote_copy(
            src_ref=pair_out.at[i], dst_ref=pair_in.at[i],
            send_sem=c_send.at[i], recv_sem=c_recv.at[i],
            device_id={"row": sibling}, device_id_type=MESH,
        )
        copy.start()
        pair_copies.append(copy)

    def y_step(i):
        pair_copies[i].wait_recv()
        part = (pair_keep[i] + pair_in[i]).reshape(depth, 2, own_rows, span)
        first, second = part[:, 0], part[:, 1]
        y_keep[i] = jnp.where(y == 0, first, second)
        y_out[i] = (
            jnp.where(y == 0, second, first).reshape(depth * own_rows, span).astype(jnp.bfloat16)
        )
        copy = pltpu.make_async_remote_copy(
            src_ref=y_out.at[i], dst_ref=y_in.at[i],
            send_sem=y_send.at[i], recv_sem=y_recv.at[i],
            device_id={"row": across}, device_id_type=MESH,
        )
        copy.start()
        y_copies.append(copy)

    def z_step(i):
        y_copies[i].wait_recv()
        part = y_keep[i] + y_in[i].astype(jnp.float32).reshape(depth, own_rows, span)
        z_keep[i] = part
        z_out[i] = part.astype(jnp.bfloat16)
        copies = []
        for k in range(1, depth):
            to = lax.rem(z + k, depth)
            copy = pltpu.make_async_remote_copy(
                src_ref=z_out.at[i, to], dst_ref=z_in.at[i, k],
                send_sem=z_send.at[i, k], recv_sem=z_recv.at[i, k],
                device_id={"row": (to * 2 + y) * 2 + c}, device_id_type=MESH,
            )
            copy.start()
            copies.append(copy)
        z_copies.append(copies)

    for t in range(chunks + 2 * lag):
        if t < chunks:
            down_step(t)
        if 0 <= t - lag < chunks:
            y_step(t - lag)
        if 0 <= t - 2 * lag < chunks:
            z_step(t - 2 * lag)
        if t == chunks + lag - 1:
            for step in range(2, depth - 1):
                f_gather.along_z(step)
                f_gather.along_y(step)

    total = jnp.zeros((own_rows, 1), jnp.float32)
    for i in range(chunks):
        part = z_keep[i, z]
        for k in range(1, depth):
            z_copies[i][k - 1].wait_recv()
            part = part + z_in[i, k].astype(jnp.float32)
        cut = slice(i * span, (i + 1) * span)
        outputs_ref[:, cut] = part.astype(jnp.bfloat16)
        miss = part - target_ref[:, cut]
        total = total + jnp.sum(miss * miss, axis=1, keepdims=True)
    loss_out[...] = jnp.broadcast_to(total / width, loss_out.shape)
    loss_copies = to_all(loss_out, loss_in, l_send, l_recv)
    f_gather.along_y(depth - 1)
    for copy in loss_copies:
        copy.wait()
    loss_in[0] = loss_out[...]

    def by_member(slot):
        return loss_in[slot]

    average = jnp.zeros((1, LANES), jnp.float32)
    for k in range(n):
        average = average + jnp.sum(loss_in[k], axis=0, keepdims=True)
    average = average / members
    spread = jnp.zeros((1, LANES), jnp.float32)
    for k in range(n):
        away = loss_in[k] - average
        spread = spread + jnp.sum(away * away, axis=0, keepdims=True)
    scale = jnp.sqrt(spread / members + 1e-06)
    for d in range(n):
        slot = lax.rem(me - d + n, n)
        all_fitness_ref[d * own_rows:(d + 1) * own_rows, :] = (
            average - loss_in[slot]
        ) / scale
    fitness_ref[...] = (average - loss_in[0]) / scale

    f_gather.finish()
    x_gather.drain()
    f_gather.drain()
    for copy in pair_copies + y_copies + [copy for some in z_copies for copy in some]:
        copy.wait_send()


def update_kernel(scale, rank, factor_ref, noise_ref, fitness_ref, update_ref, scaled):
    members = fitness_ref.shape[0]
    rows = update_ref.shape[0]

    @pl.when(pl.program_id(1) == 0)
    def _():
        fitness = fitness_ref[...]
        for r in range(rank):
            for k in range(2):
                at = (slice(r * members, (r + 1) * members), slice(k * LANES, (k + 1) * LANES))
                scaled[at] = (
                    fitness * noise_ref[(0,) + at].astype(jnp.float32)
                ).astype(jnp.bfloat16)

    start = pl.multiple_of(pl.program_id(1) * rows, LANES)
    result = jnp.dot(
        factor_ref[pl.ds(start, rows), :], scaled[...], preferred_element_type=jnp.float32
    ) * scale
    view = update_ref.reshape(2 * rows, LANES)
    view[pl.ds(0, rows, 2), :] = result[:, :LANES]
    view[pl.ds(1, rows, 2), :] = result[:, LANES:]


def fast_body(n, members_in, gate_up, down_weight, factor_in, factor_out, target):
    own_rows, width = members_in.shape
    local_units = gate_up.shape[2]
    members, rank, local_width = factor_in.shape
    blocks = local_units // LANES
    depth = n // 4
    chunks, lag = 8, 2
    span = width // chunks
    factor = factor_in.transpose(2, 1, 0).reshape(local_width, rank * members)
    rows_out = factor_out.reshape(members * rank, 2, local_units)
    bf16, f32 = jnp.bfloat16, jnp.float32
    dma = pltpu.SemaphoreType.DMA
    vmem = pl.BlockSpec(memory_space=pltpu.VMEM)
    hbm = pl.BlockSpec(memory_space=pl.ANY)
    outputs, fitness, all_fitness, full_factor, noise = pl.pallas_call(
        functools.partial(forward_kernel, n, rank, chunks, lag),
        out_shape=(
            jax.ShapeDtypeStruct((own_rows, width), bf16),
            jax.ShapeDtypeStruct((own_rows, LANES), f32),
            jax.ShapeDtypeStruct((members, LANES), f32),
            jax.ShapeDtypeStruct((n, local_width, rank * members), bf16),
            jax.ShapeDtypeStruct((blocks, rank * members, 2 * LANES), bf16),
        ),
        in_specs=[vmem, vmem, vmem, hbm, hbm, hbm],
        out_specs=(vmem, vmem, vmem, hbm, vmem),
        scratch_shapes=[
            pltpu.VMEM((blocks, width, 2, LANES), bf16),
            pltpu.VMEM((local_units, width), bf16),
            pltpu.VMEM((blocks, members * rank, 2, LANES), bf16),
            pltpu.VMEM((members * rank * 2, LANES), f32),
            pltpu.VMEM((n, own_rows, width), bf16),
            pltpu.VMEM((2 * members, 2 * width), bf16),
            pltpu.VMEM((2 * members, local_units), f32),
            pltpu.VMEM((members, local_units), bf16),
            pltpu.VMEM((n, 8, members), f32),
            pltpu.VMEM((8, members), f32),
            pltpu.VMEM((n, own_rows, LANES), f32),
            pltpu.VMEM((own_rows, LANES), f32),
            pltpu.VMEM((chunks, 2 * depth, own_rows, span), f32),
            pltpu.VMEM((chunks, 2 * depth, own_rows, span), f32),
            pltpu.VMEM((chunks, 2 * depth, own_rows, span), f32),
            pltpu.VMEM((chunks, depth * own_rows, span), bf16),
            pltpu.VMEM((chunks, depth, own_rows, span), f32),
            pltpu.VMEM((chunks, depth * own_rows, span), bf16),
            pltpu.VMEM((chunks, depth, own_rows, span), bf16),
            pltpu.VMEM((chunks, depth, own_rows, span), f32),
            pltpu.VMEM((chunks, depth, own_rows, span), bf16),
            pltpu.VMEM((8, LANES), f32),
            dma((blocks,)), dma(()), dma((blocks,)), dma((2,)),
            dma((sends_of(depth),)), dma((n,)),
            dma((sends_of(depth),)), dma((n,)),
            dma((n,)), dma((n,)), dma((n,)), dma((n,)),
            dma((chunks,)), dma((chunks,)), dma((chunks,)), dma((chunks,)),
            dma((chunks, depth)), dma((chunks, depth)),
        ],
        compiler_params=pltpu.CompilerParams(
            collective_id=0, has_side_effects=True, vmem_limit_bytes=VMEM_LIMIT
        ),
        name="forward",
    )(members_in, factor, target, gate_up, down_weight, rows_out)

    block = width
    step_scale = math.sqrt(width / (members * rank))
    update = pl.pallas_call(
        functools.partial(update_kernel, step_scale, rank),
        out_shape=jax.ShapeDtypeStruct((width, 2, local_units), f32),
        grid=(blocks, width // block),
        in_specs=[
            pl.BlockSpec((width, rank * members), lambda j, i: (0, 0)),
            pl.BlockSpec((1, rank * members, 2 * LANES), lambda j, i: (j, 0, 0)),
            pl.BlockSpec((members, LANES), lambda j, i: (0, 0)),
        ],
        out_specs=pl.BlockSpec((block, 2, LANES), lambda j, i: (i, 0, j)),
        scratch_shapes=[pltpu.VMEM((rank * members, 2 * LANES), bf16)],
        compiler_params=pltpu.CompilerParams(vmem_limit_bytes=VMEM_LIMIT),
        name="update",
    )(full_factor.reshape(width, rank * members), noise, all_fitness)
    return outputs, fitness[:, 0], update


def body(n, members_in, gate_up, down_weight, factor_in, factor_out, target):
    own_rows, width = members_in.shape
    local_units = gate_up.shape[2]
    members, rank, local_width = factor_in.shape
    aligned = local_units % LANES == 0 and local_width % LANES == 0 and members == LANES
    if aligned and n % 4 == 0 and n > 4 and own_rows == 8 and rank <= 8:
        return fast_body(n, members_in, gate_up, down_weight, factor_in, factor_out, target)
    return plain_body(members_in, gate_up, down_weight, factor_in, factor_out, target)


def plain_body(members_in, gate_up, down_weight, factor_in, factor_out, target):
    own_rows = members_in.shape[0]
    width = gate_up.shape[0]
    local_units = gate_up.shape[2]
    members = factor_in.shape[0]
    rank = factor_in.shape[1]
    whole_x = lax.all_gather(members_in, "row", axis=0, tiled=True)
    full_factor = lax.all_gather(factor_in, "row", axis=2, tiled=True)
    projected = jnp.einsum("md,mrd->mr", whole_x, full_factor, preferred_element_type=jnp.float32)
    stacked = jnp.dot(
        whole_x, gate_up.reshape(width, 2 * local_units), preferred_element_type=jnp.float32
    )
    stacked = stacked.reshape(members, 2, local_units)
    noise = jnp.sum(projected[:, :, None, None] * factor_out, axis=1)
    stacked = stacked + noise * (noise_scale / math.sqrt(rank))
    hidden = (jax.nn.silu(stacked[:, 0]) * stacked[:, 1]).astype(jnp.bfloat16)
    sums = lax.psum_scatter(
        jnp.dot(hidden, down_weight, preferred_element_type=jnp.float32),
        "row",
        scatter_dimension=0,
        tiled=True,
    )
    own_losses = jnp.mean((sums - target) ** 2, axis=1)
    losses = lax.all_gather(own_losses, "row", axis=0, tiled=True)
    average = jnp.mean(losses)
    spread = jnp.mean((losses - average) ** 2)
    all_fitness = (average - losses) / jnp.sqrt(spread + 1e-06)
    own_fitness = lax.dynamic_slice_in_dim(
        all_fitness, lax.axis_index("row") * own_rows, own_rows, 0
    )
    scaled = (all_fitness[:, None, None, None] * factor_out).astype(jnp.bfloat16)
    step_scale = math.sqrt(width / (members * rank))
    contract = (((0, 1), (0, 1)), ((), ()))
    update = lax.dot_general(full_factor, scaled, contract, preferred_element_type=jnp.float32)
    update = update * step_scale
    return (sums.astype(jnp.bfloat16), own_fitness, update)


def solution(mesh):
    return jax.shard_map(
        functools.partial(body, mesh.shape["row"]),
        mesh=mesh,
        in_specs=(
            P(("grp", "row"), None),
            P(None, None, "row"),
            P("row", None),
            P("grp", None, "row"),
            P("grp", None, None, "row"),
            P(("grp", "row"), None),
        ),
        out_specs=(P(("grp", "row"), None), P(("grp", "row")), P("grp", None, "row")),
        check_vma=False,
    )
```
